32 devices in a mesh: groups: 2 (over x), ctx: 16 (over z, y, core).
Axes of the slice: x: 2, y: 2, z: 4, core: 2. Of those that a mesh axis runs over, the one named last changes fastest.
Arguments:
- query: bfloat16 [8192, 1024], P(('groups', 'ctx')), parts along dimension 0, may hold values from -130 to 130, as said below
- key: bfloat16 [8192, 1024], P(('groups', 'ctx')), parts along dimension 0, may hold values from -4.5 to 4.5
- value: bfloat16 [8192, 1024], P(('groups', 'ctx')), parts along dimension 0, may hold values from -6 to 6
- cotangent: bfloat16 [8192, 1024], P(('groups', 'ctx')), parts along dimension 0, may hold values from -6 to 6
- global_ids: int32 [4], P('groups'), parts along dimension 0, may hold values from 0 to 63
- rand_owner: int32 [128, 6], P('groups'), parts along dimension 0, may hold values from 0 to 15, all different within a row; in each aligned block of 4 rows (0 to 3, 4 to 7, ...) at most 2 rows name the same one
- rand_local: int32 [128, 6], P('groups'), parts along dimension 0, may hold values from 0 to 3
Outputs:
- attended: bfloat16 [8192, 1024], P(('groups', 'ctx')), parts along dimension 0
- grad_query: bfloat16 [8192, 1024], P(('groups', 'ctx')), parts along dimension 0
- grad_key: bfloat16 [8192, 1024], P(('groups', 'ctx')), parts along dimension 0
- grad_value: bfloat16 [8192, 1024], P(('groups', 'ctx')), parts along dimension 0
The draws below stay inside these ranges and needn't reach their ends.
There are 2 independent parts, one for each index of `groups`. The reference program is written for one: setup_inputs(seed, part) draws one part's arguments, and reference() takes and returns one part's arrays. A program takes and returns all parts, laid end to end along the dimension named above; each array names one. Nothing has to cross between parts.
Inputs may be any that keep to these rules, and one draw needn't show every extreme that they name: query and key are drawn together. `rand_owner`: each row names 6 different devices. In the 4 rows of one device no device is named more than 2 times, and in some device's rows some device is named exactly 2 times.
All inputs are finite; a program needn't handle non-finite values.
Results may differ from the reference program's by a relative error of at most 0.017.
Values may be sent and summed in bfloat16 or wider, within the bound.
A program may use at most 192 MiB of HBM per device.

```python
import math
import jax
import jax.numpy as jnp
import numpy as np
from jax import lax

HEAD_DIM = 64
HEADS = 16
GROUP_HEADS = 8
BLOCK = 64
GLOBALS = 2
ROUNDS = 3
BLK_DEV = 4
FEAT = 1024
HG = 2
NB = 64
TOKENS = 4096
SLOT = 2
N_CTX = 16


def paired_draw(base_key):
    mixed = jax.random.fold_in(base_key, 4021)
    first, second = jax.random.split(mixed, 2)
    shape = (TOKENS, HEADS * HEAD_DIM)
    key_part = jnp.clip(jax.random.normal(first, shape, jnp.float32), -4.0, 4.0)
    query_part = jnp.clip(jax.random.normal(second, shape, jnp.float32), -4.0, 4.0)
    return (query_part, key_part)


def draw_query(key, part):
    return paired_draw(key)[0].astype(jnp.bfloat16)


def draw_key(key, part):
    return paired_draw(key)[1].astype(jnp.bfloat16)


def set_ends(array, own_key, least, high):
    longest = array.shape.index(max(array.shape))
    spots = []
    for shift in (0, 1):
        where = [jax.random.randint(jax.random.fold_in(own_key, axis), (), 0, length) for axis, length in enumerate(array.shape)]
        where[longest] = (where[longest] + shift) % array.shape[longest]
        spots.append(tuple(where))
    return array.at[spots[0]].set(least).at[spots[1]].set(high)


def steps_of(stream_key, dims, pieces, low, top_value):
    def one(dim, shards_of):
        steps = jax.random.uniform(jax.random.fold_in(jax.random.fold_in(stream_key, 6), dim), (shards_of,), jnp.float32, low / len(pieces), top_value / len(pieces))
        return jnp.repeat(jnp.exp(steps), dims[dim] // shards_of).reshape((-1,) + (1,) * (len(dims) - dim - 1))

    level = one(*pieces[0])
    for cut in pieces[1:]:
        level = level * one(*cut)
    return level


def shared_out(own_key, own, number, rows, count, top, reach, skew):
    ranking = jax.random.permutation(own_key, count)
    heavy_load, ordinary = portions_of(count, rows * top, reach, skew, True), portions_of(count, rows * top, reach, skew, False)
    places = jnp.arange(count)

    def named(sizes, rotation):
        used = int((sizes > 0).sum())
        fixed = max(1, used // 4)
        moved = fixed + (places - fixed + rotation * (used - fixed)) % max(1, count - fixed)
        return jnp.zeros((count,), jnp.int32).at[ranking[jnp.where(places < fixed, places, moved)]].set(jnp.asarray(sizes, jnp.int32))

    sizes = jnp.where(number % 4 == 0, named(heavy_load, number // 4), named(ordinary, number - number // 4 - 1))
    mixed = jax.random.permutation(jax.random.fold_in(own, 3), count)
    giver, sink = mixed[0:count // 2 * 2:2], mixed[1:count // 2 * 2:2]
    slack = jnp.minimum(sizes[giver] - 1, reach - sizes[sink]) // 2
    slack = jnp.where((giver == ranking[0]) | (sink == ranking[0]) | (sizes[sink] == 0), 0, jnp.maximum(slack, 0))
    moved = jax.random.randint(jax.random.fold_in(own, 4), (count // 2,), 0, 1 << 20) % (slack + 1)
    sizes = sizes.at[giver].add(-moved).at[sink].add(moved)
    items = jnp.searchsorted(jnp.cumsum(sizes), jnp.arange(rows * top), side="right").astype(jnp.int32)
    listing = items.reshape(top, rows).T
    listing = listing[jax.random.permutation(jax.random.fold_in(own, 1), rows)]
    rotation = jax.random.randint(jax.random.fold_in(own, 2), (rows, 1), 0, top)
    return jnp.take_along_axis(listing, (jnp.arange(top)[None, :] + rotation) % top, axis=1)


def portions_of(count, total, most, skew, full):
    portions = [(1 << 20) // math.isqrt(rank ** skew) + 1 for rank in range(1, count + 1)]
    largest = most if full else min(most, max(-(-total // count), total * portions[0] // sum(portions)))
    least = 1 if total - largest >= count - 1 else 0
    holding, rest = [largest] + [least] * (count - 1), total - largest - least * (count - 1)
    while rest > 0:
        candidates = [i for i in range(1, count) if holding[i] < largest] or [i for i in range(1, count) if holding[i] < most]
        pool, remaining = sum([portions[i] for i in candidates]), rest
        for i in candidates:
            extra = min(most - holding[i], max(1, remaining * portions[i] // pool), rest)
            holding[i] = holding[i] + extra
            rest = rest - extra
    return np.array(holding)


def bell_draw(rng, shape, width, bound, pieces=(), held_as=jnp.bfloat16):
    factor_of = steps_of(rng, shape, pieces, -0.22, 0.18) if pieces else 1.0
    values = jax.random.normal(rng, shape, jnp.float32) * width * factor_of
    return jnp.minimum(jnp.maximum(values, -bound), bound).astype(held_as)


def setup_inputs(seed: int = 0, part: int = 0) -> dict:
    arg_keys = jax.random.split(jax.random.key(seed), 8)
    own_keys = jax.random.split(jax.random.fold_in(arg_keys[7], part), 8)
    query = draw_query(jax.random.fold_in(jax.random.fold_in(arg_keys[7], part), 71), part)
    key = draw_key(jax.random.fold_in(jax.random.fold_in(arg_keys[7], part), 71), part)
    value = bell_draw(own_keys[2], (TOKENS, FEAT), 1.0, 6.0, ((0, 16),))
    cotangent = bell_draw(own_keys[3], (TOKENS, FEAT), 1.0, 6.0, ((0, 16),))
    global_ids = jax.random.randint(own_keys[4], (GLOBALS,), 0, NB).astype(jnp.int32)
    rand_owner_keys = jax.random.split(jax.random.fold_in(own_keys[5], 1), NB // BLK_DEV)
    rand_owner_turns = jax.random.permutation(jax.random.fold_in(own_keys[5], 3), NB // BLK_DEV)
    rand_owner = jax.vmap(lambda own, number: shared_out(jax.random.fold_in(own_keys[5], 2), own, number, BLK_DEV, N_CTX, HG * ROUNDS, SLOT, 2))(rand_owner_keys, rand_owner_turns).reshape((NB, HG * ROUNDS))
    rand_local = set_ends(jax.random.randint(own_keys[6], (NB, HG * ROUNDS), 0, BLK_DEV), jax.random.fold_in(own_keys[6], 1), 0, BLK_DEV - 1).astype(jnp.int32)
    return dict(query=query, key=key, value=value, cotangent=cotangent, global_ids=global_ids, rand_owner=rand_owner, rand_local=rand_local)


NEG_FILL = -1.0e30


def reference(query, key, value, cotangent, global_ids, rand_owner, rand_local):
    features = HEADS * HEAD_DIM
    groups = HEADS // GROUP_HEADS
    key_kinds = 3 + GLOBALS + ROUNDS
    key_span = key_kinds * BLOCK
    score_scale = HEAD_DIM ** -0.5
    query_five = query.reshape(NB, BLOCK, groups, GROUP_HEADS, HEAD_DIM)
    key_five = key.reshape(NB, BLOCK, groups, GROUP_HEADS, HEAD_DIM)
    value_five = value.reshape(NB, BLOCK, groups, GROUP_HEADS, HEAD_DIM)
    cot_five = cotangent.reshape(NB, BLOCK, groups, GROUP_HEADS, HEAD_DIM)
    rand_ids = (rand_owner * BLK_DEV + rand_local).astype(jnp.int32).reshape(NB, groups, ROUNDS)
    glob_ids = global_ids.astype(jnp.int32)
    group_col = jnp.arange(groups, dtype=jnp.int32)[:, None]

    def one_block(grad_pair, block_index):
        grad_k, grad_v = grad_pair
        window_raw = block_index + jnp.arange(-1, 2, dtype=jnp.int32)
        window_ok = (window_raw >= 0) & (window_raw < NB)
        window_ids = jnp.clip(window_raw, 0, NB - 1).astype(jnp.int32)
        picked = rand_ids[block_index]

        def collect(table):
            win_part = jnp.transpose(table[window_ids], (2, 3, 0, 1, 4))
            glob_part = jnp.transpose(table[glob_ids], (2, 3, 0, 1, 4))
            rand_part = jnp.transpose(table[picked, :, group_col], (0, 3, 1, 2, 4))
            joined = jnp.concatenate((win_part, glob_part, rand_part), axis=2)
            return joined.reshape(groups, GROUP_HEADS, key_span, HEAD_DIM).astype(jnp.float32)

        keys_all = collect(key_five)
        vals_all = collect(value_five)
        key_valid = jnp.concatenate((jnp.repeat(window_ok, BLOCK), jnp.ones(((GLOBALS + ROUNDS) * BLOCK,), jnp.bool_)))
        q_block = query_five[block_index].astype(jnp.float32)
        d_block = cot_five[block_index].astype(jnp.float32)
        scores = jnp.einsum('qghd,ghkd->ghqk', q_block, keys_all) * score_scale
        scores = jnp.where(key_valid, scores, NEG_FILL)
        row_max = jnp.max(scores, axis=-1, keepdims=True)
        weights = jnp.where(key_valid, jnp.exp(scores - row_max), 0.0)
        log_total = row_max + jnp.log(jnp.sum(weights, axis=-1, keepdims=True))
        probs = jnp.where(key_valid, jnp.exp(scores - log_total), 0.0)
        probs_b = probs.astype(jnp.bfloat16).astype(jnp.float32)
        attended = jnp.einsum('ghqk,ghkd->qghd', probs_b, vals_all).astype(jnp.bfloat16)
        row_dot = jnp.sum(d_block * attended.astype(jnp.float32), axis=-1)
        row_dot = jnp.transpose(row_dot, (1, 2, 0))[..., None]
        dprob = jnp.einsum('qghd,ghkd->ghqk', d_block, vals_all)
        dscore = (probs * (dprob - row_dot)).astype(jnp.bfloat16).astype(jnp.float32)
        grad_q = (jnp.einsum('ghqk,ghkd->qghd', dscore, keys_all) * score_scale).astype(jnp.bfloat16)
        term_k = jnp.einsum('ghqk,qghd->ghkd', dscore, q_block) * score_scale
        term_v = jnp.einsum('ghqk,qghd->ghkd', probs_b, d_block)

        def spread(total, term):
            term = term.reshape(groups, GROUP_HEADS, key_kinds, BLOCK, HEAD_DIM)
            win_term = jnp.transpose(term[:, :, 0:3], (2, 3, 0, 1, 4))
            glob_term = jnp.transpose(term[:, :, 3:3 + GLOBALS], (2, 3, 0, 1, 4))
            rand_term = jnp.transpose(term[:, :, 3 + GLOBALS:], (0, 2, 3, 1, 4))
            rand_term = lax.optimization_barrier(rand_term.astype(jnp.bfloat16)).astype(jnp.float32)
            total = total.at[window_ids].add(win_term)
            total = total.at[glob_ids].add(glob_term)
            total = total.at[picked, :, group_col].add(rand_term)
            return total

        return (spread(grad_k, term_k), spread(grad_v, term_v)), (attended, grad_q)

    zero_grad = jnp.zeros((NB, BLOCK, groups, GROUP_HEADS, HEAD_DIM), jnp.float32)
    grads, stacked = lax.scan(one_block, (zero_grad, zero_grad), jnp.arange(NB, dtype=jnp.int32))
    attended = stacked[0].reshape(NB * BLOCK, features)
    grad_query = stacked[1].reshape(NB * BLOCK, features)
    grad_key = grads[0].reshape(NB * BLOCK, features).astype(jnp.bfloat16)
    grad_value = grads[1].reshape(NB * BLOCK, features).astype(jnp.bfloat16)
    return attended, grad_query, grad_key, grad_value
```

```python
import functools

import jax
import jax.numpy as jnp
from jax import lax
from jax.experimental import pallas as pl
from jax.experimental.pallas import tpu as pltpu
from jax.sharding import PartitionSpec as P

HEAD_DIM = 64
GROUP_HEADS = 8
BLOCK = 64
GLOBALS = 2
ROUNDS = 3
KINDS = 3 + GLOBALS + ROUNDS
PAIR = 2 * HEAD_DIM
NEG_FILL = -1e30
SCALE = HEAD_DIM ** (-0.5)
UNROLL = 2


def pack_kernel(q_ref, k_ref, v_ref, d_ref, qd_ref, kv_ref):
    heads = kv_ref.shape[0]
    for pair in range(heads // 2):
        cols = slice(pair * PAIR, (pair + 1) * PAIR)
        for left_ref, right_ref, out_ref in ((q_ref, d_ref, qd_ref), (k_ref, v_ref, kv_ref)):
            left = left_ref[:, cols]
            right = right_ref[:, cols]
            out_ref[2 * pair] = jnp.concatenate([left[:, :HEAD_DIM], right[:, :HEAD_DIM]], axis=1)
            out_ref[2 * pair + 1] = jnp.concatenate(
                [left[:, HEAD_DIM:], right[:, HEAD_DIM:]], axis=1
            )


def unpack_kernel(qo_ref, kv_ref, att_ref, gq_ref, gk_ref, gv_ref):
    heads = kv_ref.shape[0]
    for pair in range(heads // 2):
        cols = slice(pair * PAIR, (pair + 1) * PAIR)
        for in_ref, left_ref, right_ref in ((qo_ref, gq_ref, att_ref), (kv_ref, gk_ref, gv_ref)):
            even = in_ref[2 * pair]
            odd = in_ref[2 * pair + 1]
            left_ref[:, cols] = jnp.concatenate([even[:, :HEAD_DIM], odd[:, :HEAD_DIM]], axis=1)
            right_ref[:, cols] = jnp.concatenate([even[:, HEAD_DIM:], odd[:, HEAD_DIM:]], axis=1)


def attend_kernel(query_blocks, ids_ref, edge_ref, qd_ref, kv_ref, qo_ref, gkv_ref, acc_ref):
    acc_ref[...] = jnp.zeros_like(acc_ref)
    lane = lax.broadcasted_iota(jnp.int32, (BLOCK, PAIR), 1)
    low = lane < HEAD_DIM
    row_lane = lax.broadcasted_iota(jnp.int32, (1, PAIR), 1)
    contract_last = (((1,), (1,)), ((), ()))
    contract_first = (((0,), (0,)), ((), ()))

    def front(index):
        rows = pl.ds(pl.multiple_of(index * BLOCK, BLOCK), BLOCK)
        qd = qd_ref[rows, :]
        spots = [
            pl.ds(pl.multiple_of(ids_ref[index * KINDS + kind] * BLOCK, BLOCK), BLOCK)
            for kind in range(KINDS)
        ]
        kv = jnp.concatenate([kv_ref[spot, :] for spot in spots], axis=0)
        zero = jnp.zeros_like(qd)
        diag = jnp.concatenate(
            [jnp.where(low, qd * jnp.bfloat16(SCALE), zero), jnp.where(low, zero, qd)], axis=0
        )
        both = lax.dot_general(diag, kv, contract_last, preferred_element_type=jnp.float32)
        scores = both[:BLOCK]
        dprob = both[BLOCK:]
        no_left = edge_ref[2 * index] == 1
        no_right = edge_ref[2 * index + 1] == 1
        bias = jnp.where(
            row_lane < BLOCK,
            jnp.where(no_left, NEG_FILL, 0.0),
            jnp.where(no_right, NEG_FILL, 0.0),
        ).astype(jnp.float32)
        scores = jnp.concatenate([scores[:, :PAIR] + bias, scores[:, PAIR:]], axis=1)
        row_max = jnp.max(scores, axis=1, keepdims=True)
        weights = jnp.exp(scores - row_max)
        probs = weights * (1.0 / jnp.sum(weights, axis=1, keepdims=True))
        probs_b = probs.astype(jnp.bfloat16)
        attended = jnp.dot(probs_b, kv, preferred_element_type=jnp.float32).astype(jnp.bfloat16)
        row_dot = jnp.sum(
            jnp.where(low, 0.0, qd.astype(jnp.float32) * attended.astype(jnp.float32)),
            axis=1,
            keepdims=True,
        )
        dscore = (probs * (dprob - row_dot)).astype(jnp.bfloat16)
        grad_q = jnp.dot(dscore, kv, preferred_element_type=jnp.float32) * SCALE
        qo_ref[rows, :] = jnp.where(low, grad_q.astype(jnp.bfloat16), attended)
        terms = lax.dot_general(
            jnp.concatenate([dscore, probs_b], axis=0),
            diag,
            contract_first,
            preferred_element_type=jnp.float32,
        )
        return spots, terms

    def step(number, carry):
        done = [front(number * UNROLL + part) for part in range(UNROLL)]
        for spots, terms in done:
            for kind in range(KINDS):
                acc_ref[spots[kind], :] += terms[kind * BLOCK : (kind + 1) * BLOCK]
        return carry

    lax.fori_loop(0, query_blocks // UNROLL, step, 0)
    gkv_ref[...] = acc_ref[...].astype(gkv_ref.dtype)


VMEM = pl.BlockSpec(memory_space=pltpu.VMEM)
SMEM = pl.BlockSpec(memory_space=pltpu.SMEM)


def per_device(query, key, value, cotangent, global_ids, rand_owner, rand_local):
    tokens, features = query.shape
    blocks = tokens // BLOCK
    heads = features // HEAD_DIM
    groups = heads // GROUP_HEADS
    count = lax.axis_size("ctx")
    me = lax.axis_index("ctx")
    shares = count // heads
    own_blocks = blocks // shares
    own_tokens = own_blocks * BLOCK
    all_blocks = count * blocks
    half = jax.ShapeDtypeStruct((heads, tokens, PAIR), jnp.bfloat16)
    qd, kv = pl.pallas_call(
        pack_kernel,
        out_shape=(half, half),
        in_specs=[VMEM] * 4,
        out_specs=(VMEM, VMEM),
        name="pack",
    )(query, key, value, cotangent)
    qd_send = qd.reshape(count, own_tokens, PAIR)
    kv_send = jnp.broadcast_to(kv[:, None], (heads, shares, tokens, PAIR)).reshape(
        count, tokens, PAIR
    )
    exchange = functools.partial(
        lax.all_to_all, axis_name="ctx", split_axis=0, concat_axis=0, tiled=True
    )
    kv_all = exchange(kv_send).reshape(count * tokens, PAIR)
    qd_all = exchange(qd_send).reshape(count * own_tokens, PAIR)

    my_group = me // shares // GROUP_HEADS
    share = me % shares
    picked = (rand_owner * blocks + rand_local).reshape(all_blocks, groups, ROUNDS)
    picked = lax.dynamic_index_in_dim(picked, my_group, 1, keepdims=False)
    here = jnp.arange(all_blocks, dtype=jnp.int32)
    table = jnp.concatenate(
        [
            jnp.maximum(here - 1, 0)[:, None],
            jnp.minimum(here + 1, all_blocks - 1)[:, None],
            here[:, None],
            jnp.broadcast_to(global_ids[None, :], (all_blocks, GLOBALS)),
            picked,
        ],
        axis=1,
    ).astype(jnp.int32)
    edges = jnp.stack([here == 0, here == all_blocks - 1], axis=1).astype(jnp.int32)

    def mine(array):
        split = array.reshape(count, shares, own_blocks, array.shape[1])
        return lax.dynamic_index_in_dim(split, share, 1, keepdims=False).reshape(-1)

    qo_all, gkv_all = pl.pallas_call(
        functools.partial(attend_kernel, count * own_blocks),
        out_shape=(
            jax.ShapeDtypeStruct((count * own_tokens, PAIR), jnp.bfloat16),
            jax.ShapeDtypeStruct((count * tokens, PAIR), jnp.bfloat16),
        ),
        in_specs=[SMEM, SMEM, VMEM, VMEM],
        out_specs=(VMEM, VMEM),
        scratch_shapes=[pltpu.VMEM((count * tokens, PAIR), jnp.float32)],
        compiler_params=pltpu.CompilerParams(vmem_limit_bytes=40 * 1024 * 1024),
        name="attend",
    )(mine(table), mine(edges), qd_all, kv_all)
    qo = exchange(qo_all.reshape(count, own_tokens, PAIR)).reshape(heads, tokens, PAIR)
    gkv = exchange(gkv_all.reshape(count, tokens, PAIR)).reshape(heads, shares, tokens, PAIR)
    if shares == 1:
        gkv = gkv[:, 0]
    else:
        gkv = jnp.sum(gkv.astype(jnp.float32), axis=1).astype(jnp.bfloat16)
    flat = jax.ShapeDtypeStruct((tokens, features), jnp.bfloat16)
    return pl.pallas_call(
        unpack_kernel,
        out_shape=(flat,) * 4,
        in_specs=[VMEM] * 2,
        out_specs=(VMEM,) * 4,
        name="unpack",
    )(qo, gkv)


def solution(mesh):
    rows = P(("groups", "ctx"), None)
    return jax.shard_map(
        per_device,
        mesh=mesh,
        in_specs=(rows, rows, rows, rows, P("groups"), P("groups", None), P("groups", None)),
        out_specs=(rows,) * 4,
        check_vma=False,
    )
```

```python
import functools

import jax
import jax.numpy as jnp
from jax import lax
from jax.experimental import pallas as pl
from jax.experimental.pallas import tpu as pltpu
from jax.sharding import PartitionSpec as P

HEAD_DIM = 64
GROUP_HEADS = 8
BLOCK = 64
GLOBALS = 2
ROUNDS = 3
KINDS = 3 + GLOBALS + ROUNDS
PAIR = 2 * HEAD_DIM
NEG_FILL = -1e30
SCALE = HEAD_DIM ** (-0.5)
MESH = pl.DeviceIdType.MESH


def lanes_joined(left, right):
    return jnp.concatenate([left, right], axis=1)


def greet(me, count):
    barrier = pltpu.get_barrier_semaphore()
    for step in range(1, count):
        peer = lax.rem(me + step, count)
        pl.semaphore_signal(barrier, inc=1, device_id={"ctx": peer}, device_id_type=MESH)
    return barrier


def attend_kernel(
    count,
    shares,
    ids_ref,
    q_ref,
    k_ref,
    v_ref,
    d_ref,
    qo_got,
    acc_ref,
    glob_ref,
    rand_ref,
    kv_pack,
    qd_pack,
    kv_all,
    qd_all,
    qo_put,
    kv_out,
    kv_in,
    qd_out,
    qd_in,
    qo_out,
    qo_in,
):
    me = lax.axis_index("ctx")
    heads, tokens = kv_pack.shape[:2]
    blocks = tokens // BLOCK
    own_tokens = tokens // shares
    own_blocks = own_tokens // BLOCK
    all_blocks = count * blocks
    my_share = lax.rem(me, shares)

    barrier = greet(me, count)
    for pair in range(heads // 2):
        cols = slice(pair * PAIR, (pair + 1) * PAIR)
        for left_ref, right_ref, out_ref in ((k_ref, v_ref, kv_pack), (q_ref, d_ref, qd_pack)):
            left = left_ref[:, cols]
            right = right_ref[:, cols]
            out_ref[2 * pair] = lanes_joined(left[:, :HEAD_DIM], right[:, :HEAD_DIM])
            out_ref[2 * pair + 1] = lanes_joined(left[:, HEAD_DIM:], right[:, HEAD_DIM:])
    my_head = me // shares
    my_rows = pl.ds(pl.multiple_of(my_share * own_tokens, own_tokens), own_tokens)
    for part in range(blocks):
        kv_all[me * blocks + part] = kv_pack[my_head, part * BLOCK : (part + 1) * BLOCK]
    qd_all[me] = qd_pack[my_head, my_rows, :]
    acc_ref[...] = jnp.zeros_like(acc_ref)
    glob_ref[...] = jnp.zeros_like(glob_ref)
    pl.semaphore_wait(barrier, count - 1)

    def kv_copy(dest, came):
        return pltpu.make_async_remote_copy(
            src_ref=kv_pack.at[dest // shares].reshape(blocks, BLOCK, PAIR),
            dst_ref=kv_all.at[pl.ds(came * blocks, blocks)],
            send_sem=kv_out.at[dest],
            recv_sem=kv_in.at[came],
            device_id={"ctx": dest},
            device_id_type=MESH,
        )

    def qd_copy(dest, came):
        start = pl.multiple_of(lax.rem(dest, shares) * own_tokens, own_tokens)
        return pltpu.make_async_remote_copy(
            src_ref=qd_pack.at[dest // shares, pl.ds(start, own_tokens)],
            dst_ref=qd_all.at[came],
            send_sem=qd_out.at[dest],
            recv_sem=qd_in.at[came],
            device_id={"ctx": dest},
            device_id_type=MESH,
        )

    def qo_copy(dest, came):
        return pltpu.make_async_remote_copy(
            src_ref=qo_put.at[dest],
            dst_ref=qo_got.at[came],
            send_sem=qo_out.at[dest],
            recv_sem=qo_in.at[came],
            device_id={"ctx": dest},
            device_id_type=MESH,
        )

    for make in (kv_copy, qd_copy):
        for step in range(1, count):
            make(lax.rem(me + count - step, count), me).start()
    for step in range(1, count):
        peer = lax.rem(me + step, count)
        kv_copy(peer, peer).wait_recv()

    lane = lax.broadcasted_iota(jnp.int32, (BLOCK, PAIR), 1)
    low = lane < HEAD_DIM
    row_lane = lax.broadcasted_iota(jnp.int32, (1, PAIR), 1)
    contract_last = (((1,), (1,)), ((), ()))
    contract_first = (((0,), (0,)), ((), ()))

    def front(peer, part):
        block = peer * blocks + my_share * own_blocks + part
        slot = peer * own_blocks + part
        qd = qd_all[peer, part * BLOCK : (part + 1) * BLOCK, :]
        near = [lax.rem(block + all_blocks - 1, all_blocks), lax.rem(block + 1, all_blocks), block]
        places = near + [
            ids_ref[slot * (GLOBALS + ROUNDS) + kind] for kind in range(GLOBALS + ROUNDS)
        ]
        kv = jnp.concatenate(
            [kv_all[p] for p in places], axis=0
        )
        zero = jnp.zeros_like(qd)
        diag = jnp.concatenate(
            [jnp.where(low, qd * jnp.bfloat16(SCALE), zero), jnp.where(low, zero, qd)], axis=0
        )
        both = lax.dot_general(diag, kv, contract_last, preferred_element_type=jnp.float32)
        scores = both[:BLOCK]
        dprob = both[BLOCK:]
        bias = jnp.where(
            row_lane < BLOCK,
            jnp.where(block == 0, NEG_FILL, 0.0),
            jnp.where(block == all_blocks - 1, NEG_FILL, 0.0),
        ).astype(jnp.float32)
        scores = lanes_joined(scores[:, :PAIR] + bias, scores[:, PAIR:])
        row_max = jnp.max(scores, axis=1, keepdims=True)
        weights = jnp.exp(scores - row_max)
        probs = weights * (1.0 / jnp.sum(weights, axis=1, keepdims=True))
        probs_b = probs.astype(jnp.bfloat16)
        attended = jnp.dot(probs_b, kv, preferred_element_type=jnp.float32).astype(jnp.bfloat16)
        row_dot = jnp.sum(
            jnp.where(low, 0.0, qd.astype(jnp.float32) * attended.astype(jnp.float32)),
            axis=1,
            keepdims=True,
        )
        dscore = (probs * (dprob - row_dot)).astype(jnp.bfloat16)
        grad_q = jnp.dot(dscore, kv, preferred_element_type=jnp.float32) * SCALE
        qo_put[peer, part * BLOCK : (part + 1) * BLOCK, :] = jnp.where(
            low, grad_q.astype(jnp.bfloat16), attended
        )
        terms = lax.dot_general(
            jnp.concatenate([dscore, probs_b], axis=0),
            diag,
            contract_first,
            preferred_element_type=jnp.float32,
        )
        width = ROUNDS * BLOCK
        rand_ref[pl.ds(pl.multiple_of(slot * width, width), width), :] = terms[
            (3 + GLOBALS) * BLOCK :
        ].astype(jnp.bfloat16)
        return near, terms

    def step_of(step, carry):
        peer = lax.rem(me + step, count)

        @pl.when(step > 0)
        def _():
            qd_copy(peer, peer).wait_recv()

        done = [front(peer, part) for part in range(own_blocks)]
        for near, terms in done:
            for kind in range(3):
                spot = pl.ds(pl.multiple_of(near[kind] * BLOCK, BLOCK), BLOCK)
                acc_ref[spot, :] += terms[kind * BLOCK : (kind + 1) * BLOCK]
        shared = [terms[3 * BLOCK : (3 + GLOBALS) * BLOCK] for _, terms in done]
        glob_ref[...] += functools.reduce(jnp.add, shared)

        @pl.when(step > 1)
        def _():
            qo_copy(lax.rem(me + step - 1, count), me).start()

        return carry

    lax.fori_loop(0, count, step_of, 0)
    qo_copy(lax.rem(me + count - 1, count), me).start()
    qo_got[me] = qo_put[me]
    for step in range(1, count):
        peer = lax.rem(me + step, count)
        kv_copy(peer, me).wait_send()
        qd_copy(peer, me).wait_send()
        qo_copy(peer, me).wait_send()
        qo_copy(peer, peer).wait_recv()


def sum_kernel(slots, shares, ids_ref, acc_in, glob_ref, rand_ref, qo_ref, gkv_ref, att_ref, gq_ref, acc_ref):
    acc_ref[...] = acc_in[...]
    for index in range(GLOBALS):
        spot = pl.ds(pl.multiple_of(ids_ref[index] * BLOCK, BLOCK), BLOCK)
        acc_ref[spot, :] += glob_ref[index * BLOCK : (index + 1) * BLOCK, :]

    def step(slot, carry):
        for kind in range(ROUNDS):
            place = ids_ref[slot * (GLOBALS + ROUNDS) + GLOBALS + kind]
            spot = pl.ds(pl.multiple_of(place * BLOCK, BLOCK), BLOCK)
            came = pl.ds(pl.multiple_of((slot * ROUNDS + kind) * BLOCK, BLOCK), BLOCK)
            acc_ref[spot, :] += rand_ref[came, :].astype(jnp.float32)
        return carry

    lax.fori_loop(0, slots, step, 0)
    gkv_ref[...] = acc_ref[...].astype(gkv_ref.dtype)
    own_tokens = qo_ref.shape[1]
    pairs = qo_ref.shape[0] // shares // 2
    for pair in range(pairs):
        cols = slice(pair * PAIR, (pair + 1) * PAIR)
        for share in range(shares):
            rows = slice(share * own_tokens, (share + 1) * own_tokens)
            even = qo_ref[2 * pair * shares + share]
            odd = qo_ref[(2 * pair + 1) * shares + share]
            gq_ref[rows, cols] = lanes_joined(even[:, :HEAD_DIM], odd[:, :HEAD_DIM])
            att_ref[rows, cols] = lanes_joined(even[:, HEAD_DIM:], odd[:, HEAD_DIM:])


def return_kernel(count, shares, gkv_ref, gk_ref, gv_ref, got, out_sem, in_sem):
    me = lax.axis_index("ctx")
    tokens = got.shape[1]
    barrier = greet(me, count)
    pl.semaphore_wait(barrier, count - 1)

    def copy(dest, came):
        return pltpu.make_async_remote_copy(
            src_ref=gkv_ref.at[dest],
            dst_ref=got.at[came],
            send_sem=out_sem.at[dest],
            recv_sem=in_sem.at[came],
            device_id={"ctx": dest},
            device_id_type=MESH,
        )

    for step in range(1, count):
        copy(lax.rem(me + count - step, count), me).start()
    got[me] = gkv_ref[me]
    for step in range(1, count):
        peer = lax.rem(me + step, count)
        copy(peer, me).wait_send()
        copy(peer, peer).wait_recv()

    def head_of(head):
        total = got[head * shares]
        if shares > 1:
            total = total.astype(jnp.float32)
            for share in range(1, shares):
                total += got[head * shares + share].astype(jnp.float32)
            total = total.astype(jnp.bfloat16)
        return total

    for pair in range(count // shares // 2):
        cols = slice(pair * PAIR, (pair + 1) * PAIR)
        even = head_of(2 * pair)
        odd = head_of(2 * pair + 1)
        gk_ref[:, cols] = lanes_joined(even[:, :HEAD_DIM], odd[:, :HEAD_DIM])
        gv_ref[:, cols] = lanes_joined(even[:, HEAD_DIM:], odd[:, HEAD_DIM:])


VMEM = pl.BlockSpec(memory_space=pltpu.VMEM)
SMEM = pl.BlockSpec(memory_space=pltpu.SMEM)


def per_device(query, key, value, cotangent, global_ids, rand_owner, rand_local):
    tokens, features = query.shape
    blocks = tokens // BLOCK
    heads = features // HEAD_DIM
    groups = heads // GROUP_HEADS
    count = lax.axis_size("ctx")
    me = lax.axis_index("ctx")
    shares = count // heads
    own_blocks = blocks // shares
    own_tokens = own_blocks * BLOCK
    all_blocks = count * blocks
    slots = count * own_blocks
    shape = jax.ShapeDtypeStruct
    bf16, f32 = jnp.bfloat16, jnp.float32

    my_group = me // shares // GROUP_HEADS
    picked = (rand_owner * blocks + rand_local).reshape(
        count, shares, own_blocks, groups, ROUNDS
    )
    picked = lax.dynamic_index_in_dim(picked, my_group, 3, keepdims=False)
    picked = lax.dynamic_index_in_dim(picked, me % shares, 1, keepdims=False)
    picked = picked.reshape(slots, ROUNDS)
    shared = jnp.broadcast_to(global_ids[None, :], (slots, GLOBALS))
    ids = jnp.concatenate([shared, picked], axis=1).astype(jnp.int32).reshape(-1)

    dma = pltpu.SemaphoreType.DMA((count,))
    qo, acc, glob, rand = pl.pallas_call(
        functools.partial(attend_kernel, count, shares),
        out_shape=(
            shape((count, own_tokens, PAIR), bf16),
            shape((count * tokens, PAIR), f32),
            shape((GLOBALS * BLOCK, PAIR), f32),
            shape((slots * ROUNDS * BLOCK, PAIR), bf16),
        ),
        in_specs=[SMEM] + [VMEM] * 4,
        out_specs=(VMEM,) * 4,
        scratch_shapes=[
            pltpu.VMEM((heads, tokens, PAIR), bf16),
            pltpu.VMEM((heads, tokens, PAIR), bf16),
            pltpu.VMEM((all_blocks, BLOCK, PAIR), bf16),
            pltpu.VMEM((count, own_tokens, PAIR), bf16),
            pltpu.VMEM((count, own_tokens, PAIR), bf16),
        ]
        + [dma] * 6,
        compiler_params=pltpu.CompilerParams(
            collective_id=0, has_side_effects=True, vmem_limit_bytes=40 * 1024 * 1024
        ),
        name="attend",
    )(ids, query, key, value, cotangent)
    flat = shape((tokens, features), bf16)
    gkv, attended, grad_query = pl.pallas_call(
        functools.partial(sum_kernel, slots, shares),
        out_shape=(shape((count * tokens, PAIR), bf16), flat, flat),
        in_specs=[SMEM] + [VMEM] * 4,
        out_specs=(VMEM,) * 3,
        scratch_shapes=[pltpu.VMEM((count * tokens, PAIR), f32)],
        compiler_params=pltpu.CompilerParams(vmem_limit_bytes=32 * 1024 * 1024),
        name="total",
    )(ids, acc, glob, rand, qo)
    grad_key, grad_value = pl.pallas_call(
        functools.partial(return_kernel, count, shares),
        out_shape=(flat, flat),
        in_specs=[VMEM],
        out_specs=(VMEM,) * 2,
        scratch_shapes=[pltpu.VMEM((count, tokens, PAIR), bf16), dma, dma],
        compiler_params=pltpu.CompilerParams(
            collective_id=1, has_side_effects=True, vmem_limit_bytes=16 * 1024 * 1024
        ),
        name="back",
    )(gkv.reshape(count, tokens, PAIR))
    return attended, grad_query, grad_key, grad_value


def solution(mesh):
    rows = P(("groups", "ctx"), None)
    return jax.shard_map(
        per_device,
        mesh=mesh,
        in_specs=(rows, rows, rows, rows, P("groups"), P("groups", None), P("groups", None)),
        out_specs=(rows,) * 4,
        check_vma=False,
    )
```

```python
import functools

import jax
import jax.numpy as jnp
from jax import lax
from jax.experimental import pallas as pl
from jax.experimental.pallas import tpu as pltpu
from jax.sharding import PartitionSpec as P

HEAD_DIM = 64
GROUP_HEADS = 8
BLOCK = 64
GLOBALS = 2
ROUNDS = 3
KINDS = 3 + GLOBALS + ROUNDS
PAIR = 2 * HEAD_DIM
NEG_FILL = -1e30
SCALE = HEAD_DIM ** (-0.5)
MESH = pl.DeviceIdType.MESH


def lanes_joined(left, right):
    return jnp.concatenate([left, right], axis=1)


def greet(me, count):
    barrier = pltpu.get_barrier_semaphore()
    for step in range(1, count):
        peer = lax.rem(me + step, count)
        pl.semaphore_signal(barrier, inc=1, device_id={"ctx": peer}, device_id_type=MESH)
    return barrier


def attend_kernel(
    count,
    shares,
    glob_ids,
    owner_ref,
    local_ref,
    q_hbm,
    k_hbm,
    v_hbm,
    d_hbm,
    qo_got,
    acc_ref,
    glob_ref,
    rand_ref,
    kv_pack,
    qd_pack,
    kv_all,
    qd_all,
    qo_put,
    q_ref,
    k_ref,
    v_ref,
    d_ref,
    fetch,
    kv_out,
    kv_in,
    qd_out,
    qd_in,
    qo_out,
    qo_in,
):
    me = lax.axis_index("ctx")
    heads, tokens = kv_pack.shape[:2]
    blocks = tokens // BLOCK
    own_tokens = tokens // shares
    own_blocks = own_tokens // BLOCK
    all_blocks = count * blocks
    my_share = lax.rem(me, shares)

    pulls = [
        pltpu.make_async_copy(source, target, fetch.at[index])
        for index, (source, target) in enumerate(
            ((k_hbm, k_ref), (v_hbm, v_ref), (q_hbm, q_ref), (d_hbm, d_ref))
        )
    ]
    for pull in pulls:
        pull.start()
    barrier = greet(me, count)
    my_head = me // shares
    my_group = my_head // GROUP_HEADS
    my_rows = pl.ds(pl.multiple_of(my_share * own_tokens, own_tokens), own_tokens)

    def pack(left_ref, right_ref, out_ref):
        for pair in range(heads // 2):
            cols = slice(pair * PAIR, (pair + 1) * PAIR)
            left = left_ref[:, cols]
            right = right_ref[:, cols]
            out_ref[2 * pair] = lanes_joined(left[:, :HEAD_DIM], right[:, :HEAD_DIM])
            out_ref[2 * pair + 1] = lanes_joined(left[:, HEAD_DIM:], right[:, HEAD_DIM:])

    pulls[0].wait()
    pulls[1].wait()
    pack(k_ref, v_ref, kv_pack)
    acc_ref[...] = jnp.zeros_like(acc_ref)
    glob_ref[...] = jnp.zeros_like(glob_ref)
    pl.semaphore_wait(barrier, count - 1)

    def kv_copy(dest, came):
        return pltpu.make_async_remote_copy(
            src_ref=kv_pack.at[dest // shares].reshape(blocks, BLOCK, PAIR),
            dst_ref=kv_all.at[pl.ds(came * blocks, blocks)],
            send_sem=kv_out.at[dest],
            recv_sem=kv_in.at[came],
            device_id={"ctx": dest},
            device_id_type=MESH,
        )

    def qd_copy(dest, came):
        start = pl.multiple_of(lax.rem(dest, shares) * own_tokens, own_tokens)
        return pltpu.make_async_remote_copy(
            src_ref=qd_pack.at[dest // shares, pl.ds(start, own_tokens)],
            dst_ref=qd_all.at[came],
            send_sem=qd_out.at[dest],
            recv_sem=qd_in.at[came],
            device_id={"ctx": dest},
            device_id_type=MESH,
        )

    def qo_copy(dest, came):
        return pltpu.make_async_remote_copy(
            src_ref=qo_put.at[dest],
            dst_ref=qo_got.at[came],
            send_sem=qo_out.at[dest],
            recv_sem=qo_in.at[came],
            device_id={"ctx": dest},
            device_id_type=MESH,
        )

    for step in range(1, count):
        kv_copy(lax.rem(me + count - step, count), me).start()
    for part in range(blocks):
        kv_all[me * blocks + part] = kv_pack[my_head, part * BLOCK : (part + 1) * BLOCK]
    pulls[2].wait()
    pulls[3].wait()
    pack(q_ref, d_ref, qd_pack)
    qd_all[me] = qd_pack[my_head, my_rows, :]
    for step in range(1, count):
        peer = lax.rem(me + step, count)
        kv_copy(peer, peer).wait_recv()
    for step in range(1, count):
        qd_copy(lax.rem(me + count - step, count), me).start()

    lane = lax.broadcasted_iota(jnp.int32, (BLOCK, PAIR), 1)
    low = lane < HEAD_DIM
    row_lane = lax.broadcasted_iota(jnp.int32, (1, PAIR), 1)
    contract_last = (((1,), (1,)), ((), ()))
    contract_first = (((0,), (0,)), ((), ()))

    def front(peer, part):
        block = peer * blocks + my_share * own_blocks + part
        slot = peer * own_blocks + part
        qd = qd_all[peer, part * BLOCK : (part + 1) * BLOCK, :]
        near = [lax.rem(block + all_blocks - 1, all_blocks), lax.rem(block + 1, all_blocks), block]
        places = near + [
            glob_ids[kind] for kind in range(GLOBALS)
        ] + [
            owner_ref[block, my_group * ROUNDS + kind] * blocks
            + local_ref[block, my_group * ROUNDS + kind]
            for kind in range(ROUNDS)
        ]
        kv = jnp.concatenate(
            [kv_all[p] for p in places], axis=0
        )
        zero = jnp.zeros_like(qd)
        diag = jnp.concatenate(
            [jnp.where(low, qd * jnp.bfloat16(SCALE), zero), jnp.where(low, zero, qd)], axis=0
        )
        both = lax.dot_general(diag, kv, contract_last, preferred_element_type=jnp.float32)
        scores = both[:BLOCK]
        dprob = both[BLOCK:]
        bias = jnp.where(
            row_lane < BLOCK,
            jnp.where(block == 0, NEG_FILL, 0.0),
            jnp.where(block == all_blocks - 1, NEG_FILL, 0.0),
        ).astype(jnp.float32)
        scores = lanes_joined(scores[:, :PAIR] + bias, scores[:, PAIR:])
        row_max = jnp.max(scores, axis=1, keepdims=True)
        weights = jnp.exp(scores - row_max)
        probs = weights * (1.0 / jnp.sum(weights, axis=1, keepdims=True))
        probs_b = probs.astype(jnp.bfloat16)
        attended = jnp.dot(probs_b, kv, preferred_element_type=jnp.float32).astype(jnp.bfloat16)
        row_dot = jnp.sum(
            jnp.where(low, 0.0, qd.astype(jnp.float32) * attended.astype(jnp.float32)),
            axis=1,
            keepdims=True,
        )
        dscore = (probs * (dprob - row_dot)).astype(jnp.bfloat16)
        grad_q = jnp.dot(dscore, kv, preferred_element_type=jnp.float32) * SCALE
        qo_put[peer, part * BLOCK : (part + 1) * BLOCK, :] = jnp.where(
            low, grad_q.astype(jnp.bfloat16), attended
        )
        terms = lax.dot_general(
            jnp.concatenate([dscore, probs_b], axis=0),
            diag,
            contract_first,
            preferred_element_type=jnp.float32,
        )
        width = ROUNDS * BLOCK
        rand_ref[pl.ds(pl.multiple_of(slot * width, width), width), :] = terms[
            (3 + GLOBALS) * BLOCK :
        ].astype(jnp.bfloat16)
        return near, terms

    def step_of(step, carry):
        peer = lax.rem(me + step, count)

        @pl.when(step > 0)
        def _():
            qd_copy(peer, peer).wait_recv()

        done = [front(peer, part) for part in range(own_blocks)]
        for near, terms in done:
            for kind in range(3):
                spot = pl.ds(pl.multiple_of(near[kind] * BLOCK, BLOCK), BLOCK)
                acc_ref[spot, :] += terms[kind * BLOCK : (kind + 1) * BLOCK]
        shared = [terms[3 * BLOCK : (3 + GLOBALS) * BLOCK] for _, terms in done]
        glob_ref[...] += functools.reduce(jnp.add, shared)

        @pl.when(step > 1)
        def _():
            qo_copy(lax.rem(me + step - 1, count), me).start()

        return carry

    lax.fori_loop(0, count, step_of, 0)
    qo_copy(lax.rem(me + count - 1, count), me).start()
    qo_got[me] = qo_put[me]
    for step in range(1, count):
        peer = lax.rem(me + step, count)
        kv_copy(peer, me).wait_send()
        qd_copy(peer, me).wait_send()
        qo_copy(peer, me).wait_send()
        qo_copy(peer, peer).wait_recv()


def sum_kernel(
    count,
    shares,
    blocks,
    glob_ids,
    owner_ref,
    local_ref,
    acc_in,
    glob_ref,
    rand_ref,
    qo_ref,
    gkv_ref,
    att_ref,
    gq_ref,
    acc_ref,
):
    me = lax.axis_index("ctx")
    own_blocks = blocks // shares
    first = lax.rem(me, shares) * own_blocks
    column = me // shares // GROUP_HEADS * ROUNDS
    acc_ref[...] = acc_in[...]
    for index in range(GLOBALS):
        spot = pl.ds(pl.multiple_of(glob_ids[index] * BLOCK, BLOCK), BLOCK)
        acc_ref[spot, :] += glob_ref[index * BLOCK : (index + 1) * BLOCK, :]

    def step(peer, carry):
        for part in range(own_blocks):
            block = peer * blocks + first + part
            slot = peer * own_blocks + part
            for kind in range(ROUNDS):
                place = owner_ref[block, column + kind] * blocks + local_ref[block, column + kind]
                spot = pl.ds(pl.multiple_of(place * BLOCK, BLOCK), BLOCK)
                came = pl.ds(pl.multiple_of((slot * ROUNDS + kind) * BLOCK, BLOCK), BLOCK)
                acc_ref[spot, :] += rand_ref[came, :].astype(jnp.float32)
        return carry

    lax.fori_loop(0, count, step, 0)
    gkv_ref[...] = acc_ref[...].astype(gkv_ref.dtype)
    own_tokens = qo_ref.shape[1]
    pairs = qo_ref.shape[0] // shares // 2
    for pair in range(pairs):
        cols = slice(pair * PAIR, (pair + 1) * PAIR)
        for share in range(shares):
            rows = slice(share * own_tokens, (share + 1) * own_tokens)
            even = qo_ref[2 * pair * shares + share]
            odd = qo_ref[(2 * pair + 1) * shares + share]
            gq_ref[rows, cols] = lanes_joined(even[:, :HEAD_DIM], odd[:, :HEAD_DIM])
            att_ref[rows, cols] = lanes_joined(even[:, HEAD_DIM:], odd[:, HEAD_DIM:])


def return_kernel(count, shares, gkv_ref, gk_ref, gv_ref, got, out_sem, in_sem):
    me = lax.axis_index("ctx")
    tokens = got.shape[1]
    barrier = greet(me, count)
    pl.semaphore_wait(barrier, count - 1)

    def copy(dest, came):
        return pltpu.make_async_remote_copy(
            src_ref=gkv_ref.at[dest],
            dst_ref=got.at[came],
            send_sem=out_sem.at[dest],
            recv_sem=in_sem.at[came],
            device_id={"ctx": dest},
            device_id_type=MESH,
        )

    for step in range(1, count):
        copy(lax.rem(me + count - step, count), me).start()
    got[me] = gkv_ref[me]

    def head_of(head):
        for share in range(shares):
            source = head * shares + share

            @pl.when(source != me)
            def _():
                copy(source, source).wait_recv()

        total = got[head * shares]
        if shares > 1:
            total = total.astype(jnp.float32)
            for share in range(1, shares):
                total += got[head * shares + share].astype(jnp.float32)
            total = total.astype(jnp.bfloat16)
        return total

    for pair in range(count // shares // 2):
        cols = slice(pair * PAIR, (pair + 1) * PAIR)
        even = head_of(2 * pair)
        odd = head_of(2 * pair + 1)
        gk_ref[:, cols] = lanes_joined(even[:, :HEAD_DIM], odd[:, :HEAD_DIM])
        gv_ref[:, cols] = lanes_joined(even[:, HEAD_DIM:], odd[:, HEAD_DIM:])
    for step in range(1, count):
        copy(lax.rem(me + step, count), me).wait_send()


VMEM = pl.BlockSpec(memory_space=pltpu.VMEM)
SMEM = pl.BlockSpec(memory_space=pltpu.SMEM)


def per_device(query, key, value, cotangent, global_ids, rand_owner, rand_local):
    tokens, features = query.shape
    blocks = tokens // BLOCK
    heads = features // HEAD_DIM
    count = lax.axis_size("ctx")
    shares = count // heads
    own_blocks = blocks // shares
    own_tokens = own_blocks * BLOCK
    all_blocks = count * blocks
    slots = count * own_blocks
    shape = jax.ShapeDtypeStruct
    bf16, f32 = jnp.bfloat16, jnp.float32

    dma = pltpu.SemaphoreType.DMA((count,))
    qo, acc, glob, rand = pl.pallas_call(
        functools.partial(attend_kernel, count, shares),
        out_shape=(
            shape((count, own_tokens, PAIR), bf16),
            shape((count * tokens, PAIR), f32),
            shape((GLOBALS * BLOCK, PAIR), f32),
            shape((slots * ROUNDS * BLOCK, PAIR), bf16),
        ),
        in_specs=[SMEM] * 3 + [pl.BlockSpec(memory_space=pl.ANY)] * 4,
        out_specs=(VMEM,) * 4,
        scratch_shapes=[
            pltpu.VMEM((heads, tokens, PAIR), bf16),
            pltpu.VMEM((heads, tokens, PAIR), bf16),
            pltpu.VMEM((all_blocks, BLOCK, PAIR), bf16),
            pltpu.VMEM((count, own_tokens, PAIR), bf16),
            pltpu.VMEM((count, own_tokens, PAIR), bf16),
        ]
        + [pltpu.VMEM((tokens, features), bf16)] * 4
        + [pltpu.SemaphoreType.DMA((4,))]
        + [dma] * 6,
        compiler_params=pltpu.CompilerParams(
            collective_id=0, has_side_effects=True, vmem_limit_bytes=40 * 1024 * 1024
        ),
        name="attend",
    )(global_ids, rand_owner, rand_local, query, key, value, cotangent)
    flat = shape((tokens, features), bf16)
    gkv, attended, grad_query = pl.pallas_call(
        functools.partial(sum_kernel, count, shares, blocks),
        out_shape=(shape((count * tokens, PAIR), bf16), flat, flat),
        in_specs=[SMEM] * 3 + [VMEM] * 4,
        out_specs=(VMEM,) * 3,
        scratch_shapes=[pltpu.VMEM((count * tokens, PAIR), f32)],
        compiler_params=pltpu.CompilerParams(vmem_limit_bytes=32 * 1024 * 1024),
        name="total",
    )(global_ids, rand_owner, rand_local, acc, glob, rand, qo)
    grad_key, grad_value = pl.pallas_call(
        functools.partial(return_kernel, count, shares),
        out_shape=(flat, flat),
        in_specs=[VMEM],
        out_specs=(VMEM,) * 2,
        scratch_shapes=[pltpu.VMEM((count, tokens, PAIR), bf16), dma, dma],
        compiler_params=pltpu.CompilerParams(
            collective_id=1, has_side_effects=True, vmem_limit_bytes=16 * 1024 * 1024
        ),
        name="back",
    )(gkv.reshape(count, tokens, PAIR))
    return attended, grad_query, grad_key, grad_value


def solution(mesh):
    rows = P(("groups", "ctx"), None)
    return jax.shard_map(
        per_device,
        mesh=mesh,
        in_specs=(rows, rows, rows, rows, P("groups"), P("groups", None), P("groups", None)),
        out_specs=(rows,) * 4,
        check_vma=False,
    )
```

```python
import functools

import jax
import jax.numpy as jnp
from jax import lax
from jax.experimental import pallas as pl
from jax.experimental.pallas import tpu as pltpu
from jax.sharding import PartitionSpec as P

HEAD_DIM = 64
GROUP_HEADS = 8
BLOCK = 64
GLOBALS = 2
ROUNDS = 3
KINDS = 3 + GLOBALS + ROUNDS
PAIR = 2 * HEAD_DIM
NEG_FILL = -1e30
SCALE = HEAD_DIM ** (-0.5)
MESH = pl.DeviceIdType.MESH


def lanes_joined(left, right):
    return jnp.concatenate([left, right], axis=1)


def greet(me, count):
    barrier = pltpu.get_barrier_semaphore()
    for step in range(1, count):
        peer = lax.rem(me + step, count)
        pl.semaphore_signal(barrier, inc=1, device_id={"ctx": peer}, device_id_type=MESH)
    return barrier


def attend_kernel(
    count,
    shares,
    glob_ids,
    owner_ref,
    local_ref,
    q_hbm,
    k_hbm,
    v_hbm,
    d_hbm,
    qo_got,
    acc_ref,
    glob_ref,
    rand_ref,
    kv_pack,
    qd_pack,
    kv_all,
    qd_all,
    qo_put,
    q_ref,
    k_ref,
    v_ref,
    d_ref,
    fetch,
    kv_out,
    kv_in,
    qd_out,
    qd_in,
    qo_out,
    qo_in,
):
    me = lax.axis_index("ctx")
    heads, tokens = kv_pack.shape[:2]
    blocks = tokens // BLOCK
    own_tokens = tokens // shares
    own_blocks = own_tokens // BLOCK
    all_blocks = count * blocks
    my_share = lax.rem(me, shares)

    pulls = [
        pltpu.make_async_copy(source, target, fetch.at[index])
        for index, (source, target) in enumerate(
            ((k_hbm, k_ref), (v_hbm, v_ref), (q_hbm, q_ref), (d_hbm, d_ref))
        )
    ]
    for pull in pulls:
        pull.start()
    barrier = greet(me, count)
    my_head = me // shares
    my_group = my_head // GROUP_HEADS
    my_rows = pl.ds(pl.multiple_of(my_share * own_tokens, own_tokens), own_tokens)

    def pack(left_ref, right_ref, out_ref):
        for pair in range(heads // 2):
            cols = slice(pair * PAIR, (pair + 1) * PAIR)
            left = left_ref[:, cols]
            right = right_ref[:, cols]
            out_ref[2 * pair] = lanes_joined(left[:, :HEAD_DIM], right[:, :HEAD_DIM])
            out_ref[2 * pair + 1] = lanes_joined(left[:, HEAD_DIM:], right[:, HEAD_DIM:])

    pulls[0].wait()
    pulls[1].wait()
    pack(k_ref, v_ref, kv_pack)
    acc_ref[...] = jnp.zeros_like(acc_ref)
    glob_ref[...] = jnp.zeros_like(glob_ref)
    pl.semaphore_wait(barrier, count - 1)

    def kv_copy(dest, came):
        return pltpu.make_async_remote_copy(
            src_ref=kv_pack.at[dest // shares].reshape(blocks, BLOCK, PAIR),
            dst_ref=kv_all.at[pl.ds(came * blocks, blocks)],
            send_sem=kv_out.at[dest],
            recv_sem=kv_in.at[came],
            device_id={"ctx": dest},
            device_id_type=MESH,
        )

    def qd_copy(dest, came):
        start = pl.multiple_of(lax.rem(dest, shares) * own_tokens, own_tokens)
        return pltpu.make_async_remote_copy(
            src_ref=qd_pack.at[dest // shares, pl.ds(start, own_tokens)],
            dst_ref=qd_all.at[came],
            send_sem=qd_out.at[dest],
            recv_sem=qd_in.at[came],
            device_id={"ctx": dest},
            device_id_type=MESH,
        )

    def qo_copy(dest, came):
        return pltpu.make_async_remote_copy(
            src_ref=qo_put.at[dest],
            dst_ref=qo_got.at[came],
            send_sem=qo_out.at[dest],
            recv_sem=qo_in.at[came],
            device_id={"ctx": dest},
            device_id_type=MESH,
        )

    for step in range(1, count):
        kv_copy(lax.rem(me + count - step, count), me).start()
    for part in range(blocks):
        kv_all[me * blocks + part] = kv_pack[my_head, part * BLOCK : (part + 1) * BLOCK]
    pulls[2].wait()
    pulls[3].wait()
    pack(q_ref, d_ref, qd_pack)
    qd_all[me] = qd_pack[my_head, my_rows, :]
    for step in range(1, count):
        peer = lax.rem(me + step, count)
        kv_copy(peer, peer).wait_recv()
    for step in range(1, count):
        qd_copy(lax.rem(me + count - step, count), me).start()

    lane = lax.broadcasted_iota(jnp.int32, (BLOCK, PAIR), 1)
    low = lane < HEAD_DIM
    row_lane = lax.broadcasted_iota(jnp.int32, (1, PAIR), 1)
    contract_last = (((1,), (1,)), ((), ()))
    contract_first = (((0,), (0,)), ((), ()))

    def front(peer, part):
        block = peer * blocks + my_share * own_blocks + part
        slot = peer * own_blocks + part
        qd = qd_all[peer, part * BLOCK : (part + 1) * BLOCK, :]
        near = [lax.rem(block + all_blocks - 1, all_blocks), lax.rem(block + 1, all_blocks), block]
        places = near + [
            glob_ids[kind] for kind in range(GLOBALS)
        ] + [
            owner_ref[my_group * ROUNDS + kind, block] * blocks
            + local_ref[my_group * ROUNDS + kind, block]
            for kind in range(ROUNDS)
        ]
        kv = jnp.concatenate(
            [kv_all[p] for p in places], axis=0
        )
        zero = jnp.zeros_like(qd)
        diag = jnp.concatenate(
            [jnp.where(low, qd * jnp.bfloat16(SCALE), zero), jnp.where(low, zero, qd)], axis=0
        )
        both = lax.dot_general(diag, kv, contract_last, preferred_element_type=jnp.float32)
        scores = both[:BLOCK]
        dprob = both[BLOCK:]
        bias = jnp.where(
            row_lane < BLOCK,
            jnp.where(block == 0, NEG_FILL, 0.0),
            jnp.where(block == all_blocks - 1, NEG_FILL, 0.0),
        ).astype(jnp.float32)
        scores = lanes_joined(scores[:, :PAIR] + bias, scores[:, PAIR:])
        row_max = jnp.max(scores, axis=1, keepdims=True)
        weights = jnp.exp(scores - row_max)
        probs = weights * (1.0 / jnp.sum(weights, axis=1, keepdims=True))
        probs_b = probs.astype(jnp.bfloat16)
        attended = jnp.dot(probs_b, kv, preferred_element_type=jnp.float32).astype(jnp.bfloat16)
        row_dot = jnp.sum(
            jnp.where(low, 0.0, qd.astype(jnp.float32) * attended.astype(jnp.float32)),
            axis=1,
            keepdims=True,
        )
        dscore = (probs * (dprob - row_dot)).astype(jnp.bfloat16)
        grad_q = jnp.dot(dscore, kv, preferred_element_type=jnp.float32) * SCALE
        qo_put[peer, part * BLOCK : (part + 1) * BLOCK, :] = jnp.where(
            low, grad_q.astype(jnp.bfloat16), attended
        )
        terms = lax.dot_general(
            jnp.concatenate([dscore, probs_b], axis=0),
            diag,
            contract_first,
            preferred_element_type=jnp.float32,
        )
        width = ROUNDS * BLOCK
        rand_ref[pl.ds(pl.multiple_of(slot * width, width), width), :] = terms[
            (3 + GLOBALS) * BLOCK :
        ].astype(jnp.bfloat16)
        return near, terms

    def step_of(step, carry):
        peer = lax.rem(me + step, count)

        @pl.when(step > 0)
        def _():
            qd_copy(peer, peer).wait_recv()

        done = [front(peer, part) for part in range(own_blocks)]
        for near, terms in done:
            for kind in range(3):
                spot = pl.ds(pl.multiple_of(near[kind] * BLOCK, BLOCK), BLOCK)
                acc_ref[spot, :] += terms[kind * BLOCK : (kind + 1) * BLOCK]
        shared = [terms[3 * BLOCK : (3 + GLOBALS) * BLOCK] for _, terms in done]
        glob_ref[...] += functools.reduce(jnp.add, shared)

        @pl.when(step > 1)
        def _():
            qo_copy(lax.rem(me + step - 1, count), me).start()

        return carry

    lax.fori_loop(0, count, step_of, 0)
    qo_copy(lax.rem(me + count - 1, count), me).start()
    qo_got[me] = qo_put[me]
    for step in range(1, count):
        peer = lax.rem(me + step, count)
        kv_copy(peer, me).wait_send()
        qd_copy(peer, me).wait_send()
        qo_copy(peer, me).wait_send()
        qo_copy(peer, peer).wait_recv()


def sum_kernel(
    count,
    shares,
    blocks,
    glob_ids,
    owner_ref,
    local_ref,
    acc_in,
    glob_ref,
    rand_ref,
    qo_ref,
    gkv_ref,
    att_ref,
    gq_ref,
    acc_ref,
):
    me = lax.axis_index("ctx")
    own_blocks = blocks // shares
    first = lax.rem(me, shares) * own_blocks
    column = me // shares // GROUP_HEADS * ROUNDS
    acc_ref[...] = acc_in[...]
    for index in range(GLOBALS):
        spot = pl.ds(pl.multiple_of(glob_ids[index] * BLOCK, BLOCK), BLOCK)
        acc_ref[spot, :] += glob_ref[index * BLOCK : (index + 1) * BLOCK, :]

    def step(peer, carry):
        for part in range(own_blocks):
            block = peer * blocks + first + part
            slot = peer * own_blocks + part
            for kind in range(ROUNDS):
                place = owner_ref[column + kind, block] * blocks + local_ref[column + kind, block]
                spot = pl.ds(pl.multiple_of(place * BLOCK, BLOCK), BLOCK)
                came = pl.ds(pl.multiple_of((slot * ROUNDS + kind) * BLOCK, BLOCK), BLOCK)
                acc_ref[spot, :] += rand_ref[came, :].astype(jnp.float32)
        return carry

    lax.fori_loop(0, count, step, 0)
    gkv_ref[...] = acc_ref[...].astype(gkv_ref.dtype)
    own_tokens = qo_ref.shape[1]
    pairs = qo_ref.shape[0] // shares // 2
    for pair in range(pairs):
        cols = slice(pair * PAIR, (pair + 1) * PAIR)
        for share in range(shares):
            rows = slice(share * own_tokens, (share + 1) * own_tokens)
            even = qo_ref[2 * pair * shares + share]
            odd = qo_ref[(2 * pair + 1) * shares + share]
            gq_ref[rows, cols] = lanes_joined(even[:, :HEAD_DIM], odd[:, :HEAD_DIM])
            att_ref[rows, cols] = lanes_joined(even[:, HEAD_DIM:], odd[:, HEAD_DIM:])


def return_kernel(count, shares, gkv_ref, gk_ref, gv_ref, got, out_sem, in_sem):
    me = lax.axis_index("ctx")
    tokens = got.shape[1]
    barrier = greet(me, count)
    pl.semaphore_wait(barrier, count - 1)

    def copy(dest, came):
        return pltpu.make_async_remote_copy(
            src_ref=gkv_ref.at[dest],
            dst_ref=got.at[came],
            send_sem=out_sem.at[dest],
            recv_sem=in_sem.at[came],
            device_id={"ctx": dest},
            device_id_type=MESH,
        )

    for step in range(1, count):
        copy(lax.rem(me + count - step, count), me).start()
    got[me] = gkv_ref[me]

    def head_of(head):
        for share in range(shares):
            source = head * shares + share

            @pl.when(source != me)
            def _():
                copy(source, source).wait_recv()

        total = got[head * shares]
        if shares > 1:
            total = total.astype(jnp.float32)
            for share in range(1, shares):
                total += got[head * shares + share].astype(jnp.float32)
            total = total.astype(jnp.bfloat16)
        return total

    for pair in range(count // shares // 2):
        cols = slice(pair * PAIR, (pair + 1) * PAIR)
        even = head_of(2 * pair)
        odd = head_of(2 * pair + 1)
        gk_ref[:, cols] = lanes_joined(even[:, :HEAD_DIM], odd[:, :HEAD_DIM])
        gv_ref[:, cols] = lanes_joined(even[:, HEAD_DIM:], odd[:, HEAD_DIM:])
    for step in range(1, count):
        copy(lax.rem(me + step, count), me).wait_send()


VMEM = pl.BlockSpec(memory_space=pltpu.VMEM)
SMEM = pl.BlockSpec(memory_space=pltpu.SMEM)


def per_device(query, key, value, cotangent, global_ids, rand_owner, rand_local):
    tokens, features = query.shape
    blocks = tokens // BLOCK
    heads = features // HEAD_DIM
    count = lax.axis_size("ctx")
    shares = count // heads
    own_blocks = blocks // shares
    own_tokens = own_blocks * BLOCK
    all_blocks = count * blocks
    slots = count * own_blocks
    shape = jax.ShapeDtypeStruct
    bf16, f32 = jnp.bfloat16, jnp.float32

    dma = pltpu.SemaphoreType.DMA((count,))
    qo, acc, glob, rand = pl.pallas_call(
        functools.partial(attend_kernel, count, shares),
        out_shape=(
            shape((count, own_tokens, PAIR), bf16),
            shape((count * tokens, PAIR), f32),
            shape((GLOBALS * BLOCK, PAIR), f32),
            shape((slots * ROUNDS * BLOCK, PAIR), bf16),
        ),
        in_specs=[SMEM] * 3 + [pl.BlockSpec(memory_space=pltpu.HBM)] * 4,
        out_specs=(VMEM,) * 4,
        scratch_shapes=[
            pltpu.VMEM((heads, tokens, PAIR), bf16),
            pltpu.VMEM((heads, tokens, PAIR), bf16),
            pltpu.VMEM((all_blocks, BLOCK, PAIR), bf16),
            pltpu.VMEM((count, own_tokens, PAIR), bf16),
            pltpu.VMEM((count, own_tokens, PAIR), bf16),
        ]
        + [pltpu.VMEM((tokens, features), bf16)] * 4
        + [pltpu.SemaphoreType.DMA((4,))]
        + [dma] * 6,
        compiler_params=pltpu.CompilerParams(
            collective_id=0, has_side_effects=True, vmem_limit_bytes=40 * 1024 * 1024
        ),
        name="attend",
    )(global_ids, rand_owner.T, rand_local.T, query, key, value, cotangent)
    flat = shape((tokens, features), bf16)
    gkv, attended, grad_query = pl.pallas_call(
        functools.partial(sum_kernel, count, shares, blocks),
        out_shape=(shape((count * tokens, PAIR), bf16), flat, flat),
        in_specs=[SMEM] * 3 + [VMEM] * 4,
        out_specs=(VMEM,) * 3,
        scratch_shapes=[pltpu.VMEM((count * tokens, PAIR), f32)],
        compiler_params=pltpu.CompilerParams(vmem_limit_bytes=32 * 1024 * 1024),
        name="total",
    )(global_ids, rand_owner.T, rand_local.T, acc, glob, rand, qo)
    grad_key, grad_value = pl.pallas_call(
        functools.partial(return_kernel, count, shares),
        out_shape=(flat, flat),
        in_specs=[VMEM],
        out_specs=(VMEM,) * 2,
        scratch_shapes=[pltpu.VMEM((count, tokens, PAIR), bf16), dma, dma],
        compiler_params=pltpu.CompilerParams(
            collective_id=1, has_side_effects=True, vmem_limit_bytes=16 * 1024 * 1024
        ),
        name="back",
    )(gkv.reshape(count, tokens, PAIR))
    return attended, grad_query, grad_key, grad_value


def solution(mesh):
    rows = P(("groups", "ctx"), None)
    return jax.shard_map(
        per_device,
        mesh=mesh,
        in_specs=(rows, rows, rows, rows, P("groups"), P("groups", None), P("groups", None)),
        out_specs=(rows,) * 4,
        check_vma=False,
    )
```

```python
import functools

import jax
import jax.numpy as jnp
from jax import lax
from jax.experimental import pallas as pl
from jax.experimental.pallas import tpu as pltpu
from jax.sharding import PartitionSpec as P

HEAD_DIM = 64
GROUP_HEADS = 8
BLOCK = 64
GLOBALS = 2
ROUNDS = 3
KINDS = 3 + GLOBALS + ROUNDS
PAIR = 2 * HEAD_DIM
NEG_FILL = -1e30
SCALE = HEAD_DIM ** (-0.5)
MESH = pl.DeviceIdType.MESH


def lanes_joined(left, right):
    return jnp.concatenate([left, right], axis=1)


def greet(me, count):
    barrier = pltpu.get_barrier_semaphore()
    for step in range(1, count):
        peer = lax.rem(me + step, count)
        pl.semaphore_signal(barrier, inc=1, device_id={"ctx": peer}, device_id_type=MESH)
    return barrier


def attend_kernel(
    count,
    shares,
    glob_ids,
    owner_ref,
    local_ref,
    q_hbm,
    k_hbm,
    v_hbm,
    d_hbm,
    qo_got,
    acc_ref,
    glob_ref,
    rand_ref,
    kv_pack,
    qd_pack,
    kv_all,
    qd_all,
    qo_put,
    q_ref,
    k_ref,
    v_ref,
    d_ref,
    fetch,
    kv_out,
    kv_in,
    qd_out,
    qd_in,
    qo_out,
    qo_in,
):
    me = lax.axis_index("ctx")
    heads, tokens = kv_pack.shape[:2]
    blocks = tokens // BLOCK
    own_tokens = tokens // shares
    own_blocks = own_tokens // BLOCK
    all_blocks = count * blocks
    my_share = lax.rem(me, shares)

    pulls = [
        pltpu.make_async_copy(source, target, fetch.at[index])
        for index, (source, target) in enumerate(
            ((k_hbm, k_ref), (v_hbm, v_ref), (q_hbm, q_ref), (d_hbm, d_ref))
        )
    ]
    for pull in pulls:
        pull.start()
    barrier = greet(me, count)
    my_head = me // shares
    my_group = my_head // GROUP_HEADS
    my_rows = pl.ds(pl.multiple_of(my_share * own_tokens, own_tokens), own_tokens)

    def pack(left_ref, right_ref, out_ref):
        for pair in range(heads // 2):
            cols = slice(pair * PAIR, (pair + 1) * PAIR)
            left = left_ref[:, cols]
            right = right_ref[:, cols]
            out_ref[2 * pair] = lanes_joined(left[:, :HEAD_DIM], right[:, :HEAD_DIM])
            out_ref[2 * pair + 1] = lanes_joined(left[:, HEAD_DIM:], right[:, HEAD_DIM:])

    pulls[0].wait()
    pulls[1].wait()
    pack(k_ref, v_ref, kv_pack)
    acc_ref[...] = jnp.zeros_like(acc_ref)
    glob_ref[...] = jnp.zeros_like(glob_ref)
    pl.semaphore_wait(barrier, count - 1)

    def kv_copy(dest, came):
        return pltpu.make_async_remote_copy(
            src_ref=kv_pack.at[dest // shares].reshape(blocks, BLOCK, PAIR),
            dst_ref=kv_all.at[pl.ds(came * blocks, blocks)],
            send_sem=kv_out.at[dest],
            recv_sem=kv_in.at[came],
            device_id={"ctx": dest},
            device_id_type=MESH,
        )

    def qd_copy(dest, came):
        start = pl.multiple_of(lax.rem(dest, shares) * own_tokens, own_tokens)
        return pltpu.make_async_remote_copy(
            src_ref=qd_pack.at[dest // shares, pl.ds(start, own_tokens)],
            dst_ref=qd_all.at[came],
            send_sem=qd_out.at[dest],
            recv_sem=qd_in.at[came],
            device_id={"ctx": dest},
            device_id_type=MESH,
        )

    def qo_copy(dest, came):
        return pltpu.make_async_remote_copy(
            src_ref=qo_put.at[dest],
            dst_ref=qo_got.at[came],
            send_sem=qo_out.at[dest],
            recv_sem=qo_in.at[came],
            device_id={"ctx": dest},
            device_id_type=MESH,
        )

    for step in range(1, count):
        kv_copy(lax.rem(me + count - step, count), me).start()
    for part in range(blocks):
        kv_all[me * blocks + part] = kv_pack[my_head, part * BLOCK : (part + 1) * BLOCK]
    pulls[2].wait()
    pulls[3].wait()
    pack(q_ref, d_ref, qd_pack)
    qd_all[me] = qd_pack[my_head, my_rows, :]
    for step in range(1, count):
        peer = lax.rem(me + step, count)
        kv_copy(peer, peer).wait_recv()
    for step in range(1, count):
        qd_copy(lax.rem(me + count - step, count), me).start()

    lane = lax.broadcasted_iota(jnp.int32, (BLOCK, PAIR), 1)
    low = lane < HEAD_DIM
    row_lane = lax.broadcasted_iota(jnp.int32, (1, PAIR), 1)
    contract_last = (((1,), (1,)), ((), ()))
    contract_first = (((0,), (0,)), ((), ()))

    def load(peer, part):
        block = peer * blocks + my_share * own_blocks + part
        qd = qd_all[peer, part * BLOCK : (part + 1) * BLOCK, :]
        near = [lax.rem(block + all_blocks - 1, all_blocks), lax.rem(block + 1, all_blocks), block]
        places = near + [
            glob_ids[kind] for kind in range(GLOBALS)
        ] + [
            owner_ref[my_group * ROUNDS + kind, block] * blocks
            + local_ref[my_group * ROUNDS + kind, block]
            for kind in range(ROUNDS)
        ]
        kv = jnp.concatenate([kv_all[p] for p in places], axis=0)
        zero = jnp.zeros_like(qd)
        diag = jnp.concatenate(
            [jnp.where(low, qd * jnp.bfloat16(SCALE), zero), jnp.where(low, zero, qd)], axis=0
        )
        both = lax.dot_general(diag, kv, contract_last, preferred_element_type=jnp.float32)
        return block, near, qd, kv, diag, both

    def soften(block, both):
        scores = both[:BLOCK]
        bias = jnp.where(
            row_lane < BLOCK,
            jnp.where(block == 0, NEG_FILL, 0.0),
            jnp.where(block == all_blocks - 1, NEG_FILL, 0.0),
        ).astype(jnp.float32)
        scores = lanes_joined(scores[:, :PAIR] + bias, scores[:, PAIR:])
        row_max = jnp.max(scores, axis=1, keepdims=True)
        weights = jnp.exp(scores - row_max)
        probs = weights * (1.0 / jnp.sum(weights, axis=1, keepdims=True))
        return probs, probs.astype(jnp.bfloat16)

    def finish(peer, part, qd, kv, diag, both, probs, probs_b, attended):
        slot = peer * own_blocks + part
        row_dot = jnp.sum(
            jnp.where(low, 0.0, qd.astype(jnp.float32) * attended.astype(jnp.float32)),
            axis=1,
            keepdims=True,
        )
        dscore = (probs * (both[BLOCK:] - row_dot)).astype(jnp.bfloat16)
        grad_q = jnp.dot(dscore, kv, preferred_element_type=jnp.float32) * SCALE
        qo_put[peer, part * BLOCK : (part + 1) * BLOCK, :] = jnp.where(
            low, grad_q.astype(jnp.bfloat16), attended
        )
        terms = lax.dot_general(
            jnp.concatenate([dscore, probs_b], axis=0),
            diag,
            contract_first,
            preferred_element_type=jnp.float32,
        )
        width = ROUNDS * BLOCK
        rand_ref[pl.ds(pl.multiple_of(slot * width, width), width), :] = terms[
            (3 + GLOBALS) * BLOCK :
        ].astype(jnp.bfloat16)
        return terms

    def front(peer):
        stage = [load(peer, part) for part in range(own_blocks)]
        soft = [soften(block, both) for block, _, _, _, _, both in stage]
        seen = [
            jnp.dot(probs_b, kept[3], preferred_element_type=jnp.float32).astype(jnp.bfloat16)
            for kept, (_, probs_b) in zip(stage, soft)
        ]
        return [
            (near, finish(peer, part, qd, kv, diag, both, *soft[part], seen[part]))
            for part, (block, near, qd, kv, diag, both) in enumerate(stage)
        ]

    def step_of(step, carry):
        peer = lax.rem(me + step, count)

        @pl.when(step > 0)
        def _():
            qd_copy(peer, peer).wait_recv()

        done = front(peer)
        for near, terms in done:
            for kind in range(3):
                spot = pl.ds(pl.multiple_of(near[kind] * BLOCK, BLOCK), BLOCK)
                acc_ref[spot, :] += terms[kind * BLOCK : (kind + 1) * BLOCK]
        shared = [terms[3 * BLOCK : (3 + GLOBALS) * BLOCK] for _, terms in done]
        glob_ref[...] += functools.reduce(jnp.add, shared)

        @pl.when(step > 1)
        def _():
            qo_copy(lax.rem(me + step - 1, count), me).start()

        return carry

    lax.fori_loop(0, count, step_of, 0)
    qo_copy(lax.rem(me + count - 1, count), me).start()
    qo_got[me] = qo_put[me]
    for step in range(1, count):
        peer = lax.rem(me + step, count)
        kv_copy(peer, me).wait_send()
        qd_copy(peer, me).wait_send()
        qo_copy(peer, me).wait_send()
        qo_copy(peer, peer).wait_recv()


def sum_kernel(
    count,
    shares,
    blocks,
    glob_ids,
    owner_ref,
    local_ref,
    acc_in,
    glob_ref,
    rand_ref,
    qo_ref,
    gkv_ref,
    att_ref,
    gq_ref,
    acc_ref,
):
    me = lax.axis_index("ctx")
    own_blocks = blocks // shares
    first = lax.rem(me, shares) * own_blocks
    column = me // shares // GROUP_HEADS * ROUNDS
    acc_ref[...] = acc_in[...]
    for index in range(GLOBALS):
        spot = pl.ds(pl.multiple_of(glob_ids[index] * BLOCK, BLOCK), BLOCK)
        acc_ref[spot, :] += glob_ref[index * BLOCK : (index + 1) * BLOCK, :]

    def step(peer, carry):
        for part in range(own_blocks):
            block = peer * blocks + first + part
            slot = peer * own_blocks + part
            for kind in range(ROUNDS):
                place = owner_ref[column + kind, block] * blocks + local_ref[column + kind, block]
                spot = pl.ds(pl.multiple_of(place * BLOCK, BLOCK), BLOCK)
                came = pl.ds(pl.multiple_of((slot * ROUNDS + kind) * BLOCK, BLOCK), BLOCK)
                acc_ref[spot, :] += rand_ref[came, :].astype(jnp.float32)
        return carry

    lax.fori_loop(0, count, step, 0)
    gkv_ref[...] = acc_ref[...].astype(gkv_ref.dtype)
    own_tokens = qo_ref.shape[1]
    pairs = qo_ref.shape[0] // shares // 2
    for pair in range(pairs):
        cols = slice(pair * PAIR, (pair + 1) * PAIR)
        for share in range(shares):
            rows = slice(share * own_tokens, (share + 1) * own_tokens)
            even = qo_ref[2 * pair * shares + share]
            odd = qo_ref[(2 * pair + 1) * shares + share]
            gq_ref[rows, cols] = lanes_joined(even[:, :HEAD_DIM], odd[:, :HEAD_DIM])
            att_ref[rows, cols] = lanes_joined(even[:, HEAD_DIM:], odd[:, HEAD_DIM:])


def return_kernel(count, shares, gkv_ref, gk_ref, gv_ref, got, out_sem, in_sem):
    me = lax.axis_index("ctx")
    tokens = got.shape[1]
    barrier = greet(me, count)
    pl.semaphore_wait(barrier, count - 1)

    def copy(dest, came):
        return pltpu.make_async_remote_copy(
            src_ref=gkv_ref.at[dest],
            dst_ref=got.at[came],
            send_sem=out_sem.at[dest],
            recv_sem=in_sem.at[came],
            device_id={"ctx": dest},
            device_id_type=MESH,
        )

    for step in range(1, count):
        copy(lax.rem(me + count - step, count), me).start()
    got[me] = gkv_ref[me]

    def head_of(head):
        for share in range(shares):
            source = head * shares + share

            @pl.when(source != me)
            def _():
                copy(source, source).wait_recv()

        total = got[head * shares]
        if shares > 1:
            total = total.astype(jnp.float32)
            for share in range(1, shares):
                total += got[head * shares + share].astype(jnp.float32)
            total = total.astype(jnp.bfloat16)
        return total

    for pair in range(count // shares // 2):
        cols = slice(pair * PAIR, (pair + 1) * PAIR)
        even = head_of(2 * pair)
        odd = head_of(2 * pair + 1)
        gk_ref[:, cols] = lanes_joined(even[:, :HEAD_DIM], odd[:, :HEAD_DIM])
        gv_ref[:, cols] = lanes_joined(even[:, HEAD_DIM:], odd[:, HEAD_DIM:])
    for step in range(1, count):
        copy(lax.rem(me + step, count), me).wait_send()


VMEM = pl.BlockSpec(memory_space=pltpu.VMEM)
SMEM = pl.BlockSpec(memory_space=pltpu.SMEM)


def per_device(query, key, value, cotangent, global_ids, rand_owner, rand_local):
    tokens, features = query.shape
    blocks = tokens // BLOCK
    heads = features // HEAD_DIM
    count = lax.axis_size("ctx")
    shares = count // heads
    own_blocks = blocks // shares
    own_tokens = own_blocks * BLOCK
    all_blocks = count * blocks
    slots = count * own_blocks
    shape = jax.ShapeDtypeStruct
    bf16, f32 = jnp.bfloat16, jnp.float32

    dma = pltpu.SemaphoreType.DMA((count,))
    qo, acc, glob, rand = pl.pallas_call(
        functools.partial(attend_kernel, count, shares),
        out_shape=(
            shape((count, own_tokens, PAIR), bf16),
            shape((count * tokens, PAIR), f32),
            shape((GLOBALS * BLOCK, PAIR), f32),
            shape((slots * ROUNDS * BLOCK, PAIR), bf16),
        ),
        in_specs=[SMEM] * 3 + [pl.BlockSpec(memory_space=pltpu.HBM)] * 4,
        out_specs=(VMEM,) * 4,
        scratch_shapes=[
            pltpu.VMEM((heads, tokens, PAIR), bf16),
            pltpu.VMEM((heads, tokens, PAIR), bf16),
            pltpu.VMEM((all_blocks, BLOCK, PAIR), bf16),
            pltpu.VMEM((count, own_tokens, PAIR), bf16),
            pltpu.VMEM((count, own_tokens, PAIR), bf16),
        ]
        + [pltpu.VMEM((tokens, features), bf16)] * 4
        + [pltpu.SemaphoreType.DMA((4,))]
        + [dma] * 6,
        compiler_params=pltpu.CompilerParams(
            collective_id=0, has_side_effects=True, vmem_limit_bytes=40 * 1024 * 1024
        ),
        name="attend",
    )(global_ids, rand_owner.T, rand_local.T, query, key, value, cotangent)
    flat = shape((tokens, features), bf16)
    gkv, attended, grad_query = pl.pallas_call(
        functools.partial(sum_kernel, count, shares, blocks),
        out_shape=(shape((count * tokens, PAIR), bf16), flat, flat),
        in_specs=[SMEM] * 3 + [VMEM] * 4,
        out_specs=(VMEM,) * 3,
        scratch_shapes=[pltpu.VMEM((count * tokens, PAIR), f32)],
        compiler_params=pltpu.CompilerParams(vmem_limit_bytes=32 * 1024 * 1024),
        name="total",
    )(global_ids, rand_owner.T, rand_local.T, acc, glob, rand, qo)
    grad_key, grad_value = pl.pallas_call(
        functools.partial(return_kernel, count, shares),
        out_shape=(flat, flat),
        in_specs=[VMEM],
        out_specs=(VMEM,) * 2,
        scratch_shapes=[pltpu.VMEM((count, tokens, PAIR), bf16), dma, dma],
        compiler_params=pltpu.CompilerParams(
            collective_id=1, has_side_effects=True, vmem_limit_bytes=16 * 1024 * 1024
        ),
        name="back",
    )(gkv.reshape(count, tokens, PAIR))
    return attended, grad_query, grad_key, grad_value


def solution(mesh):
    rows = P(("groups", "ctx"), None)
    return jax.shard_map(
        per_device,
        mesh=mesh,
        in_specs=(rows, rows, rows, rows, P("groups"), P("groups", None), P("groups", None)),
        out_specs=(rows,) * 4,
        check_vma=False,
    )
```
